32 devices in a mesh: space: 8 (over y, x, core), tm: 4 (over z).
Axes of the slice: x: 2, y: 2, z: 4, core: 2. Of those that a mesh axis runs over, the one named last changes fastest.
Arguments:
- state_anom: bfloat16 [4, 65536, 128], P('tm', 'space'), may hold values from -6 to 6
- obs_rows: bfloat16 [4, 16384, 128], P('tm', 'space'), may hold values from -6 to 6
- obs_weight: bfloat16 [4, 16384], P('tm', 'space'), may hold values from 0.0099487305 to 0.19921875
- innovation: bfloat16 [4, 16384], P('tm', 'space'), may hold values from -15 to 15
- obs_block: int32 [4, 16384, 1], P('tm', 'space'), may hold values from 0 to 15; in each aligned block of 2048 rows (0 to 2047, 2048 to 4095, ..., all dimensions but the last counted through in order) at most 256 rows name the same one
Outputs:
- smoothed: bfloat16 [4, 65536, 128], P('tm', 'space')
- increment: float32 [4, 65536], P('tm', 'space')
The draws below stay inside these ranges and needn't reach their ends.
Inputs may be any that keep to these rules, and one draw needn't show every extreme that they name: `obs_block`: among the 2048 observations of one device (aligned blocks of 2048 along the observation dimension) at one time, no block is named more than 256 times, and some block is named exactly 256 times.
All inputs are finite; a program needn't handle non-finite values.
Results may differ from the reference program's by a relative error of at most 0.0049.
Values may be sent and summed in bfloat16 or wider, within the bound.
A program may use at most 64 MiB of HBM per device.

```python
import math
import jax
import jax.numpy as jnp
import numpy as np
from jax import lax

M = 128
BLK_DEV = 2
OBS_DEV = 2048
NT = 4
NROWS = 65536
NOBS = 16384
NBLK = 16
CAPB = 256
RB = 4096
N_SPACE = 8


def levels(own_key, shape, shards, least, high):
    def one(position, shards_of):
        steps = jax.random.uniform(jax.random.fold_in(jax.random.fold_in(own_key, 6), position), (shards_of,), jnp.float32, least / len(shards), high / len(shards))
        return jnp.repeat(jnp.exp(steps), shape[position] // shards_of).reshape((-1,) + (1,) * (len(shape) - position - 1))

    loudness = one(*shards[0])
    for cut in shards[1:]:
        loudness = loudness * one(*cut)
    return loudness


def assign_block(key, own, number, rows, number_of, top, reach, lean):
    order = jax.random.permutation(key, number_of)
    heavy_load, ordinary = load_shares(number_of, rows * top, reach, lean, True), load_shares(number_of, rows * top, reach, lean, False)
    places = jnp.arange(number_of)

    def named(tallies, offset_by):
        used = int((tallies > 0).sum())
        fixed = max(1, used // 4)
        moved = fixed + (places - fixed + offset_by * (used - fixed)) % max(1, number_of - fixed)
        return jnp.zeros((number_of,), jnp.int32).at[order[jnp.where(places < fixed, places, moved)]].set(jnp.asarray(tallies, jnp.int32))

    tallies = jnp.where(number % 4 == 0, named(heavy_load, number // 4), named(ordinary, number - number // 4 - 1))
    mixed = jax.random.permutation(jax.random.fold_in(own, 3), number_of)
    source_of, taker = mixed[0:number_of // 2 * 2:2], mixed[1:number_of // 2 * 2:2]
    slack = jnp.minimum(tallies[source_of] - 1, reach - tallies[taker]) // 2
    slack = jnp.where((source_of == order[0]) | (taker == order[0]) | (tallies[taker] == 0), 0, jnp.maximum(slack, 0))
    moved = jax.random.randint(jax.random.fold_in(own, 4), (number_of // 2,), 0, 1 << 20) % (slack + 1)
    tallies = tallies.at[source_of].add(-moved).at[taker].add(moved)
    items = jnp.searchsorted(jnp.cumsum(tallies), jnp.arange(rows * top), side="right").astype(jnp.int32)
    grid = items.reshape(top, rows).T
    grid = grid[jax.random.permutation(jax.random.fold_in(own, 1), rows)]
    offset_by = jax.random.randint(jax.random.fold_in(own, 2), (rows, 1), 0, top)
    return jnp.take_along_axis(grid, (jnp.arange(top)[None, :] + offset_by) % top, axis=1)


def load_shares(count, total, limit, skew, full):
    loads = [(1 << 20) // math.isqrt(standing ** skew) + 1 for standing in range(1, count + 1)]
    largest = limit if full else min(limit, max(-(-total // count), total * loads[0] // sum(loads)))
    least = 1 if total - largest >= count - 1 else 0
    given, rest = [largest] + [least] * (count - 1), total - largest - least * (count - 1)
    while rest > 0:
        free = [i for i in range(1, count) if given[i] < largest] or [i for i in range(1, count) if given[i] < limit]
        whole, left = sum([loads[i] for i in free]), rest
        for i in free:
            more = min(limit - given[i], max(1, left * loads[i] // whole), rest)
            given[i] = given[i] + more
            rest = rest - more
    return np.array(given)


def centred(rng, extent, scale, bound, shards=(), kind=jnp.bfloat16):
    result = jax.random.normal(rng, extent, jnp.float32) * scale
    if len(shards) > 0:
        result = levels(rng, extent, shards, -0.22, 0.18) * result
    return jnp.clip(result, min=-bound, max=bound).astype(kind)


def setup_inputs(seed: int = 0) -> dict:
    keys = jax.random.split(jax.random.key(seed), 6)
    state_anom = centred(keys[0], (NT, NROWS, M), 1.0, 6.0, ((0, 4), (1, 8)))
    obs_rows = centred(keys[1], (NT, NOBS, M), 1.0, 6.0, ((0, 4), (1, 8)))
    obs_weight = jnp.clip(jnp.exp(math.log(0.19921875) - 2.9969585 * jax.random.uniform(keys[2], (NT, NOBS), jnp.float32) ** levels(keys[2], (NT, NOBS), ((0, 4), (1, 8)), -0.2, 0.2)), 0.0099487305, 0.19921875).astype(jnp.bfloat16)
    innovation = centred(keys[3], (NT, NOBS), 3.0, 15.0, ((0, 4), (1, 8)))
    obs_block_keys = jax.random.split(jax.random.fold_in(keys[4], 1), NT * NOBS // OBS_DEV)
    obs_block_turns = jax.random.permutation(jax.random.fold_in(keys[4], 3), NT * NOBS // OBS_DEV)
    obs_block = jax.vmap(lambda own, number: assign_block(jax.random.fold_in(keys[4], 2), own, number, OBS_DEV, NBLK, 1, CAPB, 2))(obs_block_keys, obs_block_turns).reshape((NT, NOBS, 1))
    return dict(state_anom=state_anom, obs_rows=obs_rows, obs_weight=obs_weight, innovation=innovation, obs_block=obs_block)


def place_rows(block, rows, weight, innov, nblk, capb):
    count = block.shape[0]
    order = jnp.argsort(block, stable=True)
    sorted_block = block[order]
    labels = jnp.arange(nblk, dtype=jnp.int32)
    counts = lax.optimization_barrier(jnp.sum((block[:, None] == labels[None, :]).astype(jnp.int32), axis=0))
    starts = jnp.cumsum(counts) - counts
    rank = jnp.arange(count, dtype=jnp.int32) - starts[sorted_block]
    slot = (sorted_block * capb + rank).astype(jnp.int32)
    width = rows.shape[1]
    rows_buf = jnp.zeros((nblk * capb, width), rows.dtype).at[slot].set(rows[order])
    weight_buf = jnp.zeros((nblk * capb,), weight.dtype).at[slot].set(weight[order])
    innov_buf = jnp.zeros((nblk * capb,), innov.dtype).at[slot].set(innov[order])
    return (rows_buf, weight_buf, innov_buf)

def make_transforms(gram, drive, members):
    eye = jnp.eye(members, dtype=gram.dtype)
    system = 0.5 * (gram + jnp.swapaxes(gram, 1, 2)) + (members - 1.0) * eye
    lower = jnp.linalg.cholesky(system)
    eye_all = jnp.broadcast_to(eye, system.shape)
    inv_lower = jax.scipy.linalg.solve_triangular(lower, eye_all, lower=True)
    transform = jnp.sqrt(members - 1.0) * jnp.swapaxes(inv_lower, 1, 2)
    inner = jnp.einsum('bij,bj->bi', inv_lower, drive, precision=lax.Precision.HIGHEST)
    shift = jnp.einsum('bji,bj->bi', inv_lower, inner, precision=lax.Precision.HIGHEST)
    return (transform, shift)

def reference(state_anom, obs_rows, obs_weight, innovation, obs_block):
    nblk = BLK_DEV * N_SPACE
    capb = CAPB

    def per_time(packed):
        rows_t, weight_t, innov_t, block_t = packed
        rows_s = rows_t.reshape(N_SPACE, OBS_DEV, M)
        weight_s = weight_t.reshape(N_SPACE, OBS_DEV)
        innov_s = innov_t.reshape(N_SPACE, OBS_DEV)
        block_s = block_t.reshape(N_SPACE, OBS_DEV)
        placed = jax.vmap(lambda b, r, w, d: place_rows(b, r, w, d, nblk, capb))(block_s, rows_s, weight_s, innov_s)
        rows_buf = placed[0].reshape(N_SPACE, nblk, capb, M)
        weight_buf = placed[1].reshape(N_SPACE, nblk, capb).astype(jnp.float32)
        innov_buf = placed[2].reshape(N_SPACE, nblk, capb).astype(jnp.float32)
        rows_wide = rows_buf.astype(jnp.float32)
        scaled = (weight_buf[..., None] * rows_wide).astype(jnp.bfloat16)
        gram = jnp.einsum('sbcm,sbcn->bmn', scaled.astype(jnp.float32), rows_wide)
        drive = jnp.einsum('sbc,sbcm->bm', weight_buf * innov_buf, rows_wide, precision=lax.Precision.HIGHEST)
        return make_transforms(gram, drive, M)
    transform_all, shift_all = lax.map(per_time, (obs_rows, obs_weight, innovation, obs_block[:, :, 0]))
    total = jnp.broadcast_to(jnp.eye(M, dtype=jnp.float32), (nblk, M, M))
    offset = jnp.zeros((nblk, M), jnp.float32)
    totals = [None] * NT
    offsets = [None] * NT
    for step in range(NT - 1, -1, -1):
        offset = shift_all[step] + jnp.einsum('bij,bj->bi', transform_all[step], offset, precision=lax.Precision.HIGHEST)
        total = jnp.einsum('bij,bjk->bik', transform_all[step], total, precision=lax.Precision.HIGHEST)
        totals[step] = total
        offsets[step] = offset
    smoothed_list = []
    increment_list = []
    for step in range(NT):
        anom = state_anom[step].reshape(nblk, RB, M).astype(jnp.float32)
        total_low = totals[step].astype(jnp.bfloat16).astype(jnp.float32)
        offset_low = offsets[step].astype(jnp.bfloat16).astype(jnp.float32)
        smoothed_list.append(jnp.einsum('brm,bmn->brn', anom, total_low).astype(jnp.bfloat16).reshape(NROWS, M))
        increment_list.append(jnp.einsum('brm,bm->br', anom, offset_low).reshape(NROWS))
    return (jnp.stack(smoothed_list), jnp.stack(increment_list))
```

```python
import functools
import math

import jax
import jax.numpy as jnp
from jax import lax
from jax.experimental import pallas as pl
from jax.experimental.pallas import tpu as pltpu
from jax.sharding import PartitionSpec as P

BLK_DEV = 2
PAD = 8
GRANT = 24 * 1024 * 1024
GRAM_GRANT = 64696320
MESH = pl.DeviceIdType.MESH
NT_DIMS = (((1,), (1,)), ((), ()))


def partner(me, k, n):
    out, bit = 0, 1
    while bit < n:
        out = out + bit * ((me // bit + k // bit) % 2)
        bit *= 2
    return out


def steps(low, high, body):
    if high - low <= 16:
        for k in range(low, high):
            body(k)
    else:
        lax.fori_loop(low, high, lambda k, c: (body(k), c)[1], 0)


def fold(gram, two):
    half = gram.shape[0] // 2
    wide = gram.shape[1]
    row = lax.broadcasted_iota(jnp.int32, (half, wide), 0)
    lane = lax.broadcasted_iota(jnp.int32, (half, wide), 1)
    low = gram[half:, :]
    main = jnp.where((lane > row) & (lane < half), pltpu.roll(low, half, 1), gram[0:half, :])
    diag = jnp.sum(jnp.where(lane == row + half, low, 0.0), axis=0, keepdims=True)
    return main, jnp.where(lax.broadcasted_iota(jnp.int32, (PAD, wide), 0) == PAD - 1, diag, two)


def gram_kernel(n, rows_hbm, weight_hbm, innov_hbm, block_hbm, anom_ref, out_ref, anom_out, anom_sem, rows_ref, weight_ref, innov_ref, block_ref, in_sem, scaled, drv, right, near, own, near_in, far_in, send_sem, recv_sem):
    loads = [
        pltpu.make_async_copy(src, dst, in_sem.at[i])
        for i, (src, dst) in enumerate(
            ((rows_hbm, rows_ref), (weight_hbm, weight_ref), (innov_hbm, innov_ref), (block_hbm, block_ref))
        )
    ]
    for load in loads:
        load.start()
    me = lax.axis_index("space")
    members = rows_ref.shape[1]
    half = members // 2
    chips = n // 2
    barrier = pltpu.get_barrier_semaphore()

    def greet(k):
        pl.semaphore_signal(barrier, inc=1, device_id={"space": partner(me, k, n)}, device_id_type=MESH)

    greet(1)
    steps(1, chips, lambda q: greet(2 * q))
    fetch = pltpu.make_async_copy(anom_ref, anom_out, anom_sem)
    fetch.start()
    for load in loads:
        load.wait()
    weight = weight_ref[...].astype(jnp.float32)
    rows_t = rows_ref[...].astype(jnp.float32).T
    scaled[...] = (weight * rows_t).astype(jnp.bfloat16)
    rows_t = rows_t.astype(jnp.bfloat16)
    for h in range(BLK_DEV):
        pick = jnp.where(block_ref[...] % BLK_DEV == h, 1.0, 0.0).astype(jnp.bfloat16)
        right[members * h:members * (h + 1), :] = rows_t * pick
    weighted = weight * innov_ref[...].astype(jnp.float32)
    high = weighted.astype(jnp.bfloat16)
    low = (weighted - high.astype(jnp.float32)).astype(jnp.bfloat16)
    drv[...] = jnp.concatenate(
        [high.astype(jnp.float32), low.astype(jnp.float32), jnp.zeros((2 * PAD - 2, high.shape[1]), jnp.float32)], axis=0
    ).astype(jnp.bfloat16)

    def parts(devs):
        lhs = []
        for dev in devs:
            mask = jnp.where(block_ref[...] // BLK_DEV == dev, 1.0, 0.0).astype(jnp.bfloat16)
            lhs = lhs + [scaled[...] * mask, drv[...] * mask]
        both = lax.dot_general(jnp.concatenate(lhs, axis=0), right[...], NT_DIMS, preferred_element_type=jnp.float32)
        for i in range(len(devs)):
            at = i * (members + 2 * PAD)
            yield [
                fold(both[at:at + members, members * h:members * (h + 1)],
                     both[at + members:at + members + PAD, members * h:members * (h + 1)])
                for h in range(BLK_DEV)
            ]

    def near_copy(q):
        return pltpu.make_async_remote_copy(
            src_ref=near.at[q], dst_ref=near_in.at[q], send_sem=send_sem.at[0, q], recv_sem=recv_sem.at[0, q],
            device_id={"space": partner(me, 1, n)}, device_id_type=MESH,
        )

    def far_copy(q):
        return pltpu.make_async_remote_copy(
            src_ref=own.at[q], dst_ref=far_in.at[q], send_sem=send_sem.at[1, q], recv_sem=recv_sem.at[1, q],
            device_id={"space": partner(me, 2 * q, n)}, device_id_type=MESH,
        )

    def work(q):
        for place, part in zip((near, own), parts((partner(me, 2 * q + 1, n), partner(me, 2 * q, n)))):
            for h, (main, rest) in enumerate(part):
                place[q, h, 0:half, :] = main
                place[q, h, half:, :] = rest

    def relay(q):
        near_copy(q).wait()
        own[q] = own[q] + near_in[q]
        far_copy(q).start()

    work(chips - 1)
    pl.semaphore_wait(barrier, chips)
    near_copy(chips - 1).start()

    def advance(turn):
        q = chips - 1 - turn
        work(q)
        near_copy(q).start()
        relay(q + 1)

    steps(1, chips, advance)
    near_copy(0).wait()
    out_ref[...] = own[0] + near_in[0]

    def take(turn):
        q = chips - turn
        far_copy(q).wait()
        out_ref[...] += far_in[q]

    steps(1, chips, take)
    fetch.wait()


def factor_kernel(n, sums_ref, total_ref, offset_ref, acc, off, tri, vec, tri_in, vec_in, send_sem, recv_sem):
    here = lax.axis_index("tm")
    barrier = pltpu.get_barrier_semaphore()

    def greet(k):
        pl.semaphore_signal(barrier, inc=1, device_id={"tm": (here + k) % n}, device_id_type=MESH)

    steps(1, n, greet)
    members = tri.shape[1]
    half = members // 2
    groups = members // 8
    lane = lax.broadcasted_iota(jnp.int32, (8, members), 1)
    sub_wide = lax.broadcasted_iota(jnp.int32, (8, members), 0)
    row = lax.broadcasted_iota(jnp.int32, (members, members), 0)
    col = lax.broadcasted_iota(jnp.int32, (members, members), 1)
    work, drive = [], []
    for h in range(BLK_DEV):
        main = sums_ref[h, 0:half, :]
        rest = sums_ref[h, half:, :]
        r0, c0 = row[0:half, :], col[0:half, :]
        top = jnp.where((c0 < r0) | (c0 >= half), main, 0.0)
        bottom = jnp.where(c0 > r0 + half, pltpu.roll(main, half, 1), 0.0)
        part = jnp.concatenate([top, bottom], axis=0)
        first = jnp.concatenate([main, jnp.broadcast_to(rest[PAD - 1:PAD, :], (half, members))], axis=0)
        system = part + part.T + jnp.where(row == col, first + (members - 1.0), 0.0)
        work.append([system[8 * g:8 * g + 8, :] for g in range(groups)])
        drive.append(rest[0:1, :] + rest[1:2, :])
    inverse = [[], []]
    for g0 in range(groups):
        base = 8 * g0
        place = sub_wide + base
        panel = (lane >= base) & (lane < base + 8)
        for h in range(BLK_DEV):
            w = work[h]
            z = jnp.where(panel, jnp.where(lane == place, 1.0, 0.0), w[g0])
            cols = [jnp.broadcast_to(w[g0][:, base + q:base + q + 1], (8, members)) for q in range(8)]
            kept, pivots = z, cols[0]
            for q in range(8):
                here_row = sub_wide == q
                kept = jnp.where(here_row, z, kept)
                pivots = jnp.where(here_row, cols[q], pivots)
                factor = jnp.where(here_row, 0.0, cols[q] * (1.0 / cols[q][q:q + 1, :]))
                z = z - factor * z[q:q + 1, :]
                for p in range(q + 1, 8):
                    cols[p] = cols[p] - factor * cols[p][q:q + 1, :]
            z = z * (1.0 / pivots)
            inverse[h].append(jnp.where(lane <= place, kept, 0.0) * lax.rsqrt(pivots))
            if g0 + 1 == groups:
                continue
            fresh = jnp.where(panel, 0.0, w[g0 + 1])
            for q in range(8):
                fresh = fresh - w[g0 + 1][:, base + q:base + q + 1] * z[q:q + 1, :]
            if g0 + 2 < groups:
                rest = jnp.concatenate(w[g0 + 2:], axis=0)
                wide = (col >= base)[0:members - base - 16, :] & (col < base + 8)[0:members - base - 16, :]
                deep = jnp.concatenate([jnp.zeros((8, members), jnp.float32)] * g0 + [z] + [jnp.zeros((8, members), jnp.float32)] * (groups - g0 - 1), axis=0)
                moved = jnp.dot(jnp.where(wide, rest, 0.0), deep, precision=lax.Precision.HIGHEST, preferred_element_type=jnp.float32)
                rest = jnp.where(wide, 0.0, rest) - moved
                for g in range(g0 + 2, groups):
                    w[g] = rest[8 * (g - g0 - 2):8 * (g - g0 - 1), :]
            w[g0 + 1] = fresh
    scale = math.sqrt(members - 1.0)
    packed, lines = jnp.zeros((members, members), jnp.float32), []
    for h in range(BLK_DEV):
        x = jnp.concatenate(inverse[h], axis=0)
        inner = jnp.sum(x * drive[h], axis=1, keepdims=True)
        shift = jnp.sum(x * inner, axis=0, keepdims=True)
        flip = x.T
        packed = packed + jnp.where(col < row, x, 0.0) if h == 0 else packed + jnp.where(col > row, flip, 0.0)
        lines = lines + [jnp.sum(jnp.where(row == col, x, 0.0), axis=0, keepdims=True), shift]
        acc[h] = scale * flip
        off[h] = jnp.sum(jnp.where(row == col, jnp.broadcast_to(shift, (members, members)), 0.0), axis=1, keepdims=True)
    tri[...] = packed.astype(jnp.bfloat16)
    vec[...] = jnp.concatenate(lines + [jnp.zeros((PAD - 2 * BLK_DEV, members), jnp.float32)], axis=0)
    pl.semaphore_wait(barrier, n - 1)

    def copies(k):
        peer = {"tm": (here + n - k) % n}
        return (
            pltpu.make_async_remote_copy(
                src_ref=tri, dst_ref=tri_in.at[k], send_sem=send_sem.at[0, k], recv_sem=recv_sem.at[0, k],
                device_id=peer, device_id_type=MESH,
            ),
            pltpu.make_async_remote_copy(
                src_ref=vec, dst_ref=vec_in.at[k], send_sem=send_sem.at[1, k], recv_sem=recv_sem.at[1, k],
                device_id=peer, device_id_type=MESH,
            ),
        )

    def push(k):
        @pl.when(here >= k)
        def _():
            for copy in copies(k):
                copy.start()

    steps(1, n, lambda turn: push(n - turn))

    def take(k):
        @pl.when(here + k < n)
        def _():
            for copy in copies(k):
                copy.wait_recv()
            got = tri_in[k].astype(jnp.float32)
            for h in range(BLK_DEV):
                before = acc[h]
                diag = vec_in[k, 2 * h:2 * h + 1, :]
                shift = vec_in[k, 2 * h + 1:2 * h + 2, :]
                off[h] = off[h] + jnp.sum(before * shift, axis=1, keepdims=True)
                high = before.astype(jnp.bfloat16)
                low = (before - high.astype(jnp.float32)).astype(jnp.bfloat16)
                pair = jnp.concatenate([high, low], axis=0)
                if h == 0:
                    side = jnp.where(col < row, got, 0.0).astype(jnp.bfloat16)
                    both = lax.dot_general(pair, side, NT_DIMS, preferred_element_type=jnp.float32)
                else:
                    side = jnp.where(col > row, got, 0.0).astype(jnp.bfloat16)
                    both = jnp.dot(pair, side, preferred_element_type=jnp.float32)
                acc[h] = scale * (before * diag + both[0:members, :] + both[members:, :])

    steps(1, n, take)

    def settle(k):
        @pl.when(here >= k)
        def _():
            for copy in copies(k):
                copy.wait_send()

    steps(1, n, settle)
    for h in range(BLK_DEV):
        total_ref[h] = acc[h].astype(jnp.bfloat16)
        spread = jnp.where(row == col, jnp.broadcast_to(off[h], (members, members)), 0.0)
        line = jnp.sum(spread, axis=0, keepdims=True)
        offset_ref[h] = jnp.broadcast_to(line, (16, members)).astype(jnp.bfloat16)


def apply_kernel(anom_ref, total_ref, offset_ref, smooth_ref, inc_ref, smooth, inc, sems):
    rows_dev = anom_ref.shape[1]
    tiles = 8
    tile = rows_dev // tiles
    out = []
    for i in range(tiles):
        h = i * BLK_DEV // tiles
        cut = slice(i * tile, (i + 1) * tile)
        anom = anom_ref[0, cut, :]
        smooth[0, cut, :] = jnp.dot(anom, total_ref[h], preferred_element_type=jnp.float32).astype(jnp.bfloat16)
        copy = pltpu.make_async_copy(smooth.at[:, cut, :], smooth_ref.at[:, cut, :], sems.at[i])
        copy.start()
        out.append(copy)
        part = lax.dot_general(offset_ref[h], anom, NT_DIMS, preferred_element_type=jnp.float32)
        inc[:, cut] = part[0:1, :]
    copy = pltpu.make_async_copy(inc, inc_ref, sems.at[tiles])
    copy.start()
    for copy in out + [copy]:
        copy.wait()


def body(state_anom, obs_rows, obs_weight, innovation, obs_block):
    count, members = obs_rows.shape[1:]
    n_space = lax.axis_size("space")
    n_time = lax.axis_size("tm")
    wide = members // 2 + PAD
    vmem = pl.BlockSpec(memory_space=pltpu.VMEM)
    sums, anom = pl.pallas_call(
        functools.partial(gram_kernel, n_space),
        out_shape=(
            pltpu.VMEM((BLK_DEV, wide, members), jnp.float32),
            pltpu.VMEM(state_anom.shape, state_anom.dtype),
        ),
        in_specs=[pl.BlockSpec(memory_space=pltpu.MemorySpace.HBM)] * 5,
        out_specs=(vmem, vmem),
        scratch_shapes=[
            pltpu.SemaphoreType.DMA(()),
            pltpu.VMEM((count, members), obs_rows.dtype),
            pltpu.VMEM((1, count), obs_weight.dtype),
            pltpu.VMEM((1, count), innovation.dtype),
            pltpu.VMEM((1, count), obs_block.dtype),
            pltpu.SemaphoreType.DMA((4,)),
            pltpu.VMEM((members, count), jnp.bfloat16),
            pltpu.VMEM((2 * PAD, count), jnp.bfloat16),
            pltpu.VMEM((BLK_DEV * members, count), jnp.bfloat16),
            *[pltpu.VMEM((n_space // 2, BLK_DEV, wide, members), jnp.float32)] * 4,
            pltpu.SemaphoreType.DMA((2, n_space // 2)),
            pltpu.SemaphoreType.DMA((2, n_space // 2)),
        ],
        compiler_params=pltpu.CompilerParams(collective_id=0, has_side_effects=True, vmem_limit_bytes=GRAM_GRANT),
        name="gram",
    )(obs_rows[0], obs_weight, innovation, obs_block.reshape(1, count), state_anom)
    total, offset = pl.pallas_call(
        functools.partial(factor_kernel, n_time),
        out_shape=(
            pltpu.VMEM((BLK_DEV, members, members), jnp.bfloat16),
            pltpu.VMEM((BLK_DEV, 16, members), jnp.bfloat16),
        ),
        in_specs=[vmem],
        out_specs=(vmem, vmem),
        scratch_shapes=[
            pltpu.VMEM((BLK_DEV, members, members), jnp.float32),
            pltpu.VMEM((BLK_DEV, members, 1), jnp.float32),
            pltpu.VMEM((members, members), jnp.bfloat16),
            pltpu.VMEM((PAD, members), jnp.float32),
            pltpu.VMEM((n_time, members, members), jnp.bfloat16),
            pltpu.VMEM((n_time, PAD, members), jnp.float32),
            pltpu.SemaphoreType.DMA((2, n_time)),
            pltpu.SemaphoreType.DMA((2, n_time)),
        ],
        compiler_params=pltpu.CompilerParams(collective_id=1, has_side_effects=True, vmem_limit_bytes=GRANT),
        name="factor",
    )(pltpu.with_memory_space_constraint(sums, pltpu.MemorySpace.VMEM))
    rows_dev = state_anom.shape[1]
    any_spec = pl.BlockSpec(memory_space=pl.ANY)
    return pl.pallas_call(
        apply_kernel,
        out_shape=(
            jax.ShapeDtypeStruct((1, rows_dev, members), jnp.bfloat16),
            jax.ShapeDtypeStruct((1, rows_dev), jnp.float32),
        ),
        in_specs=[vmem] * 3,
        out_specs=(any_spec, any_spec),
        scratch_shapes=[
            pltpu.VMEM((1, rows_dev, members), jnp.bfloat16),
            pltpu.VMEM((1, rows_dev), jnp.float32),
            pltpu.SemaphoreType.DMA((9,)),
        ],
        compiler_params=pltpu.CompilerParams(vmem_limit_bytes=GRANT),
        name="apply",
    )(*[pltpu.with_memory_space_constraint(x, pltpu.MemorySpace.VMEM) for x in (anom, total, offset)])


def solution(mesh):
    placed = (
        P("tm", "space", None),
        P("tm", "space", None),
        P("tm", "space"),
        P("tm", "space"),
        P("tm", "space", None),
    )
    return jax.shard_map(
        body,
        mesh=mesh,
        in_specs=placed,
        out_specs=(P("tm", "space", None), P("tm", "space")),
        check_vma=False,
    )
```

```python
import functools
import math

import jax
import jax.numpy as jnp
from jax import lax
from jax.experimental import pallas as pl
from jax.experimental.pallas import tpu as pltpu
from jax.sharding import PartitionSpec as P

BLK_DEV = 2
PAD = 8
GRANT = 24 * 1024 * 1024
GRAM_GRANT = 64696320
MESH = pl.DeviceIdType.MESH
NT_DIMS = (((1,), (1,)), ((), ()))


def partner(me, k, n):
    out, bit = 0, 1
    while bit < n:
        out = out + bit * ((me // bit + k // bit) % 2)
        bit *= 2
    return out


def steps(low, high, body):
    if high - low <= 16:
        for k in range(low, high):
            body(k)
    else:
        lax.fori_loop(low, high, lambda k, c: (body(k), c)[1], 0)


def fold(both, members):
    row = lax.broadcasted_iota(jnp.int32, (members, members), 0)
    col = lax.broadcasted_iota(jnp.int32, (members, members), 1)
    one, two = both[0:members, 0:members], both[0:members, members:]
    diag = jnp.sum(jnp.where(row == col, two, 0.0), axis=0, keepdims=True)
    place = lax.broadcasted_iota(jnp.int32, (PAD, members), 0)
    drives = both[members:members + PAD, :]
    rest = jnp.where(place < 2, drives[:, 0:members], jnp.where(place < 4, pltpu.roll(drives[:, members:], 2, 0), diag))
    return jnp.where(col > row, two, one), rest


def gram_kernel(n, rows_hbm, weight_hbm, innov_hbm, block_hbm, anom_ref, out_ref, anom_out, anom_sem, rows_ref, weight_ref, innov_ref, block_ref, in_sem, scaled, drv, right, near, own, near_in, far_in, send_sem, recv_sem):
    loads = [
        pltpu.make_async_copy(src, dst, in_sem.at[i])
        for i, (src, dst) in enumerate(
            ((rows_hbm, rows_ref), (weight_hbm, weight_ref), (innov_hbm, innov_ref), (block_hbm, block_ref))
        )
    ]
    for load in loads:
        load.start()
    me = lax.axis_index("space")
    members = rows_ref.shape[1]
    chips = n // 2
    barrier = pltpu.get_barrier_semaphore()

    def greet(k):
        pl.semaphore_signal(barrier, inc=1, device_id={"space": partner(me, k, n)}, device_id_type=MESH)

    greet(1)
    steps(1, chips, lambda q: greet(2 * q))
    fetch = pltpu.make_async_copy(anom_ref, anom_out, anom_sem)
    fetch.start()
    for load in loads:
        load.wait()
    weight = weight_ref[...].astype(jnp.float32)
    rows_t = rows_ref[...].astype(jnp.float32).T
    scaled[...] = (weight * rows_t).astype(jnp.bfloat16)
    rows_t = rows_t.astype(jnp.bfloat16)
    for h in range(BLK_DEV):
        pick = jnp.where(block_ref[...] % BLK_DEV == h, 1.0, 0.0).astype(jnp.bfloat16)
        right[members * h:members * (h + 1), :] = rows_t * pick
    weighted = weight * innov_ref[...].astype(jnp.float32)
    high = weighted.astype(jnp.bfloat16)
    low = (weighted - high.astype(jnp.float32)).astype(jnp.bfloat16)
    drv[...] = jnp.concatenate(
        [high.astype(jnp.float32), low.astype(jnp.float32), jnp.zeros((2 * PAD - 2, high.shape[1]), jnp.float32)], axis=0
    ).astype(jnp.bfloat16)

    def parts(devs):
        lhs = []
        for dev in devs:
            mask = jnp.where(block_ref[...] // BLK_DEV == dev, 1.0, 0.0).astype(jnp.bfloat16)
            lhs = lhs + [scaled[...] * mask, drv[...] * mask]
        both = lax.dot_general(jnp.concatenate(lhs, axis=0), right[...], NT_DIMS, preferred_element_type=jnp.float32)
        for i in range(len(devs)):
            at = i * (members + 2 * PAD)
            yield fold(both[at:at + members + PAD, :], members)

    def near_copy(q):
        return pltpu.make_async_remote_copy(
            src_ref=near.at[q], dst_ref=near_in.at[q], send_sem=send_sem.at[0, q], recv_sem=recv_sem.at[0, q],
            device_id={"space": partner(me, 1, n)}, device_id_type=MESH,
        )

    def far_copy(q):
        return pltpu.make_async_remote_copy(
            src_ref=own.at[q], dst_ref=far_in.at[q], send_sem=send_sem.at[1, q], recv_sem=recv_sem.at[1, q],
            device_id={"space": partner(me, 2 * q, n)}, device_id_type=MESH,
        )

    def work(q):
        for place, part in zip((near, own), parts((partner(me, 2 * q + 1, n), partner(me, 2 * q, n)))):
            place[q, 0:members, :] = part[0]
            place[q, members:, :] = part[1]

    def relay(q):
        near_copy(q).wait()
        own[q] = own[q] + near_in[q]
        far_copy(q).start()

    work(chips - 1)
    pl.semaphore_wait(barrier, chips)
    near_copy(chips - 1).start()

    def advance(turn):
        q = chips - 1 - turn
        work(q)
        near_copy(q).start()
        if chips > 16:
            relay(q + 1)
        elif turn > 1:
            relay(q + 2)

    steps(1, chips, advance)
    if 1 < chips <= 16:
        relay(1)
    near_copy(0).wait()
    out_ref[...] = own[0] + near_in[0]

    def take(turn):
        q = chips - turn
        far_copy(q).wait()
        out_ref[...] += far_in[q]

    steps(1, chips, take)
    fetch.wait()


def factor_kernel(n, sums_ref, total_ref, offset_ref, acc, off, tri, vec, tri_in, vec_in, send_sem, recv_sem):
    here = lax.axis_index("tm")
    barrier = pltpu.get_barrier_semaphore()

    def greet(k):
        pl.semaphore_signal(barrier, inc=1, device_id={"tm": (here + k) % n}, device_id_type=MESH)

    steps(1, n, greet)
    members = tri.shape[1]
    groups = members // 8
    lane = lax.broadcasted_iota(jnp.int32, (8, members), 1)
    sub_wide = lax.broadcasted_iota(jnp.int32, (8, members), 0)
    row = lax.broadcasted_iota(jnp.int32, (members, members), 0)
    col = lax.broadcasted_iota(jnp.int32, (members, members), 1)
    main, rest = sums_ref[0:members, :], sums_ref[members:, :]
    main_t = main.T
    work, drive = [], []
    for h in range(BLK_DEV):
        keep = col < row if h == 0 else col > row
        line = main if h == 0 else jnp.broadcast_to(rest[2 * BLK_DEV:2 * BLK_DEV + 1, :], (members, members))
        system = jnp.where(row == col, line + (members - 1.0), jnp.where(keep, main, main_t))
        work.append([system[8 * g:8 * g + 8, :] for g in range(groups)])
        drive.append(rest[2 * h:2 * h + 1, :] + rest[2 * h + 1:2 * h + 2, :])
    inverse = [[] for _ in range(BLK_DEV)]
    head = [None] * BLK_DEV
    for g0 in range(groups):
        base = 8 * g0
        first = g0 % 2 == 0
        place = sub_wide + base
        panel = (lane >= base) & (lane < base + 8)

        def drop(target, z):
            terms = [target[:, base + q:base + q + 1] * z[q:q + 1, :] for q in range(8)]
            while len(terms) > 1:
                terms = [terms[i] + terms[i + 1] for i in range(0, len(terms), 2)]
            return jnp.where(panel, 0.0, target) - terms[0]

        for h in range(BLK_DEV):
            w = work[h]
            z = jnp.where(panel, jnp.where(lane == place, 1.0, 0.0), w[g0])
            cols = [jnp.broadcast_to(w[g0][:, base + q:base + q + 1], (8, members)) for q in range(8)]
            kept, pivots = z, cols[0]
            for q in range(8):
                here_row = sub_wide == q
                kept = jnp.where(here_row, z, kept)
                pivots = jnp.where(here_row, cols[q], pivots)
                factor = jnp.where(here_row, 0.0, cols[q]) * (1.0 / cols[q][q:q + 1, :])
                z = z - factor * z[q:q + 1, :]
                for p in range(q + 1, 8):
                    cols[p] = cols[p] - factor * cols[p][q:q + 1, :]
            z = z * (1.0 / pivots)
            inverse[h].append(jnp.where(lane <= place, kept, 0.0) * lax.rsqrt(pivots))
            near = range(g0 + 1, min(groups, g0 + (4 if first else 3)))
            old = w[g0 + 3:]
            if first:
                head[h] = z
            elif old:
                rest = jnp.concatenate(old, axis=0)
                count = rest.shape[0]
                wide = (col >= base - 8)[0:count, :] & (col < base + 8)[0:count, :]
                above = [jnp.zeros((8, members), jnp.float32)] * (g0 - 1)
                below = [jnp.zeros((8, members), jnp.float32)] * (groups - g0 - 1)
                deep = jnp.concatenate(above + [drop(head[h], z), z] + below, axis=0)
                moved = jnp.dot(jnp.where(wide, rest, 0.0), deep, precision=lax.Precision.HIGHEST, preferred_element_type=jnp.float32)
                rest = jnp.where(wide, 0.0, rest) - moved
            for g in near:
                w[g] = drop(w[g], z)
            if not first and old:
                for g in range(g0 + 3, groups):
                    w[g] = rest[8 * (g - g0 - 3):8 * (g - g0 - 2), :]
    scale = math.sqrt(members - 1.0)
    packed, lines = jnp.zeros((members, members), jnp.float32), []
    for h in range(BLK_DEV):
        x = jnp.concatenate(inverse[h], axis=0)
        inner = jnp.sum(x * drive[h], axis=1, keepdims=True)
        shift = jnp.sum(x * inner, axis=0, keepdims=True)
        flip = x.T
        packed = packed + jnp.where(col < row, x, 0.0) if h == 0 else packed + jnp.where(col > row, flip, 0.0)
        lines = lines + [jnp.sum(jnp.where(row == col, x, 0.0), axis=0, keepdims=True), shift]
        acc[h] = scale * flip
        off[h] = jnp.sum(jnp.where(row == col, jnp.broadcast_to(shift, (members, members)), 0.0), axis=1, keepdims=True)
    tri[...] = packed.astype(jnp.bfloat16)
    vec[...] = jnp.concatenate(lines + [jnp.zeros((PAD - 2 * BLK_DEV, members), jnp.float32)], axis=0)
    pl.semaphore_wait(barrier, n - 1)

    def copies(k):
        peer = {"tm": (here + n - k) % n}
        return (
            pltpu.make_async_remote_copy(
                src_ref=tri, dst_ref=tri_in.at[k], send_sem=send_sem.at[0, k], recv_sem=recv_sem.at[0, k],
                device_id=peer, device_id_type=MESH,
            ),
            pltpu.make_async_remote_copy(
                src_ref=vec, dst_ref=vec_in.at[k], send_sem=send_sem.at[1, k], recv_sem=recv_sem.at[1, k],
                device_id=peer, device_id_type=MESH,
            ),
        )

    def push(k):
        @pl.when(here >= k)
        def _():
            for copy in copies(k):
                copy.start()

    steps(1, n, lambda turn: push(n - turn))

    def take(k):
        @pl.when(here + k < n)
        def _():
            for copy in copies(k):
                copy.wait_recv()
            got = tri_in[k].astype(jnp.float32)
            for h in range(BLK_DEV):
                before = acc[h]
                diag = vec_in[k, 2 * h:2 * h + 1, :]
                shift = vec_in[k, 2 * h + 1:2 * h + 2, :]
                off[h] = off[h] + jnp.sum(before * shift, axis=1, keepdims=True)
                high = before.astype(jnp.bfloat16)
                low = (before - high.astype(jnp.float32)).astype(jnp.bfloat16)
                pair = jnp.concatenate([high, low], axis=0)
                if h == 0:
                    side = jnp.where(col < row, got, 0.0).astype(jnp.bfloat16)
                    both = lax.dot_general(pair, side, NT_DIMS, preferred_element_type=jnp.float32)
                else:
                    side = jnp.where(col > row, got, 0.0).astype(jnp.bfloat16)
                    both = jnp.dot(pair, side, preferred_element_type=jnp.float32)
                acc[h] = scale * (before * diag + both[0:members, :] + both[members:, :])

    steps(1, n, take)

    def settle(k):
        @pl.when(here >= k)
        def _():
            for copy in copies(k):
                copy.wait_send()

    steps(1, n, settle)
    for h in range(BLK_DEV):
        total_ref[h] = acc[h].astype(jnp.bfloat16)
        spread = jnp.where(row == col, jnp.broadcast_to(off[h], (members, members)), 0.0)
        line = jnp.sum(spread, axis=0, keepdims=True)
        offset_ref[h] = jnp.broadcast_to(line, (16, members)).astype(jnp.bfloat16)


def apply_kernel(anom_ref, total_ref, offset_ref, smooth_ref, inc_ref, smooth, inc, sems):
    rows_dev = anom_ref.shape[1]
    tiles = 8
    tile = rows_dev // tiles
    out = []
    for i in range(tiles):
        h = i * BLK_DEV // tiles
        cut = slice(i * tile, (i + 1) * tile)
        anom = anom_ref[0, cut, :]
        smooth[0, cut, :] = jnp.dot(anom, total_ref[h], preferred_element_type=jnp.float32).astype(jnp.bfloat16)
        copy = pltpu.make_async_copy(smooth.at[:, cut, :], smooth_ref.at[:, cut, :], sems.at[i])
        copy.start()
        out.append(copy)
        part = lax.dot_general(offset_ref[h], anom, NT_DIMS, preferred_element_type=jnp.float32)
        inc[:, cut] = part[0:1, :]
    copy = pltpu.make_async_copy(inc, inc_ref, sems.at[tiles])
    copy.start()
    for copy in out + [copy]:
        copy.wait()


def body(state_anom, obs_rows, obs_weight, innovation, obs_block):
    count, members = obs_rows.shape[1:]
    n_space = lax.axis_size("space")
    n_time = lax.axis_size("tm")
    wide = members + PAD
    vmem = pl.BlockSpec(memory_space=pltpu.VMEM)
    sums, anom = pl.pallas_call(
        functools.partial(gram_kernel, n_space),
        out_shape=(
            pltpu.VMEM((wide, members), jnp.float32),
            pltpu.VMEM(state_anom.shape, state_anom.dtype),
        ),
        in_specs=[pl.BlockSpec(memory_space=pltpu.MemorySpace.HBM)] * 5,
        out_specs=(vmem, vmem),
        scratch_shapes=[
            pltpu.SemaphoreType.DMA(()),
            pltpu.VMEM((count, members), obs_rows.dtype),
            pltpu.VMEM((1, count), obs_weight.dtype),
            pltpu.VMEM((1, count), innovation.dtype),
            pltpu.VMEM((1, count), obs_block.dtype),
            pltpu.SemaphoreType.DMA((4,)),
            pltpu.VMEM((members, count), jnp.bfloat16),
            pltpu.VMEM((2 * PAD, count), jnp.bfloat16),
            pltpu.VMEM((BLK_DEV * members, count), jnp.bfloat16),
            *[pltpu.VMEM((n_space // 2, wide, members), jnp.float32)] * 4,
            pltpu.SemaphoreType.DMA((2, n_space // 2)),
            pltpu.SemaphoreType.DMA((2, n_space // 2)),
        ],
        compiler_params=pltpu.CompilerParams(collective_id=0, has_side_effects=True, vmem_limit_bytes=GRAM_GRANT),
        name="gram",
    )(obs_rows[0], obs_weight, innovation, obs_block.reshape(1, count), state_anom)
    total, offset = pl.pallas_call(
        functools.partial(factor_kernel, n_time),
        out_shape=(
            pltpu.VMEM((BLK_DEV, members, members), jnp.bfloat16),
            pltpu.VMEM((BLK_DEV, 16, members), jnp.bfloat16),
        ),
        in_specs=[vmem],
        out_specs=(vmem, vmem),
        scratch_shapes=[
            pltpu.VMEM((BLK_DEV, members, members), jnp.float32),
            pltpu.VMEM((BLK_DEV, members, 1), jnp.float32),
            pltpu.VMEM((members, members), jnp.bfloat16),
            pltpu.VMEM((PAD, members), jnp.float32),
            pltpu.VMEM((n_time, members, members), jnp.bfloat16),
            pltpu.VMEM((n_time, PAD, members), jnp.float32),
            pltpu.SemaphoreType.DMA((2, n_time)),
            pltpu.SemaphoreType.DMA((2, n_time)),
        ],
        compiler_params=pltpu.CompilerParams(collective_id=1, has_side_effects=True, vmem_limit_bytes=GRANT),
        name="factor",
    )(pltpu.with_memory_space_constraint(sums, pltpu.MemorySpace.VMEM))
    rows_dev = state_anom.shape[1]
    any_spec = pl.BlockSpec(memory_space=pl.ANY)
    return pl.pallas_call(
        apply_kernel,
        out_shape=(
            jax.ShapeDtypeStruct((1, rows_dev, members), jnp.bfloat16),
            jax.ShapeDtypeStruct((1, rows_dev), jnp.float32),
        ),
        in_specs=[vmem] * 3,
        out_specs=(any_spec, any_spec),
        scratch_shapes=[
            pltpu.VMEM((1, rows_dev, members), jnp.bfloat16),
            pltpu.VMEM((1, rows_dev), jnp.float32),
            pltpu.SemaphoreType.DMA((9,)),
        ],
        compiler_params=pltpu.CompilerParams(vmem_limit_bytes=GRANT),
        name="apply",
    )(*[pltpu.with_memory_space_constraint(x, pltpu.MemorySpace.VMEM) for x in (anom, total, offset)])


def solution(mesh):
    placed = (
        P("tm", "space", None),
        P("tm", "space", None),
        P("tm", "space"),
        P("tm", "space"),
        P("tm", "space", None),
    )
    return jax.shard_map(
        body,
        mesh=mesh,
        in_specs=placed,
        out_specs=(P("tm", "space", None), P("tm", "space")),
        check_vma=False,
    )
```

```python
import functools
import math

import jax
import jax.numpy as jnp
from jax import lax
from jax.experimental import pallas as pl
from jax.experimental.pallas import tpu as pltpu
from jax.sharding import PartitionSpec as P

BLK_DEV = 2
PAD = 8
GRANT = 24 * 1024 * 1024
GRAM_GRANT = 64696320
MESH = pl.DeviceIdType.MESH
NT_DIMS = (((1,), (1,)), ((), ()))


def partner(me, k, n):
    out, bit = 0, 1
    while bit < n:
        out = out + bit * ((me // bit + k // bit) % 2)
        bit *= 2
    return out


def steps(low, high, body):
    if high - low <= 16:
        for k in range(low, high):
            body(k)
    else:
        lax.fori_loop(low, high, lambda k, c: (body(k), c)[1], 0)


def fold(both, members):
    row = lax.broadcasted_iota(jnp.int32, (members, members), 0)
    col = lax.broadcasted_iota(jnp.int32, (members, members), 1)
    one, two = both[0:members, 0:members], both[0:members, members:]
    diag = jnp.sum(jnp.where(row == col, two, 0.0), axis=0, keepdims=True)
    place = lax.broadcasted_iota(jnp.int32, (PAD, members), 0)
    drives = both[members:members + PAD, :]
    rest = jnp.where(place < 2, drives[:, 0:members], jnp.where(place < 4, pltpu.roll(drives[:, members:], 2, 0), diag))
    return jnp.where(col > row, two, one), rest


def gram_kernel(n, rows_hbm, weight_hbm, innov_hbm, block_hbm, anom_ref, out_ref, anom_out, anom_sem, rows_ref, weight_ref, innov_ref, block_ref, in_sem, scaled, drv, right, near, own, near_in, far_in, send_sem, recv_sem):
    loads = [
        pltpu.make_async_copy(src, dst, in_sem.at[i])
        for i, (src, dst) in enumerate(
            ((rows_hbm, rows_ref), (weight_hbm, weight_ref), (innov_hbm, innov_ref), (block_hbm, block_ref))
        )
    ]
    for load in loads:
        load.start()
    me = lax.axis_index("space")
    members = rows_ref.shape[1]
    chips = n // 2
    barrier = pltpu.get_barrier_semaphore()

    def greet(k):
        pl.semaphore_signal(barrier, inc=1, device_id={"space": partner(me, k, n)}, device_id_type=MESH)

    greet(1)
    steps(1, chips, lambda q: greet(2 * q))
    fetch = pltpu.make_async_copy(anom_ref, anom_out, anom_sem)
    fetch.start()
    for load in loads:
        load.wait()
    weight = weight_ref[...].astype(jnp.float32)
    rows_t = rows_ref[...].T
    scaled[...] = (weight * rows_t.astype(jnp.float32)).astype(jnp.bfloat16)
    for h in range(BLK_DEV):
        pick = jnp.where(block_ref[...] % BLK_DEV == h, 1.0, 0.0).astype(jnp.bfloat16)
        right[members * h:members * (h + 1), :] = rows_t * pick
    weighted = weight * innov_ref[...].astype(jnp.float32)
    high = weighted.astype(jnp.bfloat16)
    low = (weighted - high.astype(jnp.float32)).astype(jnp.bfloat16)
    drv[...] = jnp.concatenate(
        [high.astype(jnp.float32), low.astype(jnp.float32), jnp.zeros((2 * PAD - 2, high.shape[1]), jnp.float32)], axis=0
    ).astype(jnp.bfloat16)

    def parts(devs):
        lhs = []
        for dev in devs:
            mask = jnp.where(block_ref[...] // BLK_DEV == dev, 1.0, 0.0).astype(jnp.bfloat16)
            lhs = lhs + [scaled[...] * mask, drv[...] * mask]
        both = lax.dot_general(jnp.concatenate(lhs, axis=0), right[...], NT_DIMS, preferred_element_type=jnp.float32)
        for i in range(len(devs)):
            at = i * (members + 2 * PAD)
            yield fold(both[at:at + members + PAD, :], members)

    def near_copy(q):
        return pltpu.make_async_remote_copy(
            src_ref=near.at[q], dst_ref=near_in.at[q], send_sem=send_sem.at[0, q], recv_sem=recv_sem.at[0, q],
            device_id={"space": partner(me, 1, n)}, device_id_type=MESH,
        )

    def far_copy(q):
        return pltpu.make_async_remote_copy(
            src_ref=own.at[q], dst_ref=far_in.at[q], send_sem=send_sem.at[1, q], recv_sem=recv_sem.at[1, q],
            device_id={"space": partner(me, 2 * q, n)}, device_id_type=MESH,
        )

    def work(q):
        for place, part in zip((near, own), parts((partner(me, 2 * q + 1, n), partner(me, 2 * q, n)))):
            place[q, 0:members, :] = part[0]
            place[q, members:, :] = part[1]

    def relay(q):
        near_copy(q).wait()
        own[q] = own[q] + near_in[q]
        far_copy(q).start()

    work(chips - 1)
    pl.semaphore_wait(barrier, chips)
    near_copy(chips - 1).start()

    def advance(turn):
        q = chips - 1 - turn
        work(q)
        near_copy(q).start()
        if chips > 16:
            relay(q + 1)
        elif turn > 1:
            relay(q + 2)

    steps(1, chips, advance)
    if 1 < chips <= 16:
        relay(1)
    near_copy(0).wait()
    out_ref[...] = own[0] + near_in[0]

    def take(turn):
        q = chips - turn
        far_copy(q).wait()
        out_ref[...] += far_in[q]

    steps(1, chips, take)
    fetch.wait()


def factor_kernel(n, sums_ref, total_ref, offset_ref, acc, off, tri, vec, tri_in, vec_in, send_sem, recv_sem):
    here = lax.axis_index("tm")
    barrier = pltpu.get_barrier_semaphore()

    def greet(k):
        pl.semaphore_signal(barrier, inc=1, device_id={"tm": (here + k) % n}, device_id_type=MESH)

    steps(1, n, greet)
    members = tri.shape[1]
    groups = members // 8
    lane = lax.broadcasted_iota(jnp.int32, (8, members), 1)
    sub_wide = lax.broadcasted_iota(jnp.int32, (8, members), 0)
    row = lax.broadcasted_iota(jnp.int32, (members, members), 0)
    col = lax.broadcasted_iota(jnp.int32, (members, members), 1)
    main, rest = sums_ref[0:members, :], sums_ref[members:, :]
    main_t = main.T
    work, drive = [], []
    for h in range(BLK_DEV):
        keep = col < row if h == 0 else col > row
        line = main if h == 0 else jnp.broadcast_to(rest[2 * BLK_DEV:2 * BLK_DEV + 1, :], (members, members))
        system = jnp.where(row == col, line + (members - 1.0), jnp.where(keep, main, main_t))
        work.append([system[8 * g:8 * g + 8, :] for g in range(groups)])
        drive.append(rest[2 * h:2 * h + 1, :] + rest[2 * h + 1:2 * h + 2, :])
    inverse = [[] for _ in range(BLK_DEV)]
    head = [None] * BLK_DEV
    for g0 in range(groups):
        base = 8 * g0
        first = g0 % 2 == 0
        place = sub_wide + base
        panel = (lane >= base) & (lane < base + 8)

        def drop(target, z):
            terms = [target[:, base + q:base + q + 1] * z[q:q + 1, :] for q in range(8)]
            while len(terms) > 1:
                terms = [terms[i] + terms[i + 1] for i in range(0, len(terms), 2)]
            return jnp.where(panel, 0.0, target) - terms[0]

        for h in range(BLK_DEV):
            w = work[h]
            z = jnp.where(panel, jnp.where(lane == place, 1.0, 0.0), w[g0])
            cols = [jnp.broadcast_to(w[g0][:, base + q:base + q + 1], (8, members)) for q in range(8)]
            kept, pivots = z, cols[0]
            for q in range(8):
                here_row = sub_wide == q
                kept = jnp.where(here_row, z, kept)
                pivots = jnp.where(here_row, cols[q], pivots)
                factor = jnp.where(here_row, 0.0, cols[q]) * (1.0 / cols[q][q:q + 1, :])
                z = z - factor * z[q:q + 1, :]
                for p in range(q + 1, 8):
                    cols[p] = cols[p] - factor * cols[p][q:q + 1, :]
            z = z * (1.0 / pivots)
            inverse[h].append(jnp.where(lane <= place, kept, 0.0) * lax.rsqrt(pivots))
            near = range(g0 + 1, min(groups, g0 + (4 if first else 3)))
            old = w[g0 + 3:]
            if first:
                head[h] = z
            elif old:
                rest = jnp.concatenate(old, axis=0)
                count = rest.shape[0]
                wide = (col >= base - 8)[0:count, :] & (col < base + 8)[0:count, :]
                above = [jnp.zeros((8, members), jnp.float32)] * (g0 - 1)
                below = [jnp.zeros((8, members), jnp.float32)] * (groups - g0 - 1)
                deep = jnp.concatenate(above + [drop(head[h], z), z] + below, axis=0)
                moved = jnp.dot(jnp.where(wide, rest, 0.0), deep, precision=lax.Precision.HIGHEST, preferred_element_type=jnp.float32)
                rest = jnp.where(wide, 0.0, rest) - moved
            for g in near:
                w[g] = drop(w[g], z)
            if not first and old:
                for g in range(g0 + 3, groups):
                    w[g] = rest[8 * (g - g0 - 3):8 * (g - g0 - 2), :]
    scale = math.sqrt(members - 1.0)
    packed, lines = jnp.zeros((members, members), jnp.float32), []
    for h in range(BLK_DEV):
        x = jnp.concatenate(inverse[h], axis=0)
        inner = jnp.sum(x * drive[h], axis=1, keepdims=True)
        shift = jnp.sum(x * inner, axis=0, keepdims=True)
        flip = x.T
        packed = packed + jnp.where(col < row, x, 0.0) if h == 0 else packed + jnp.where(col > row, flip, 0.0)
        lines = lines + [jnp.sum(jnp.where(row == col, x, 0.0), axis=0, keepdims=True), shift]
        acc[h] = scale * flip
        off[h] = jnp.sum(jnp.where(row == col, jnp.broadcast_to(shift, (members, members)), 0.0), axis=1, keepdims=True)
    tri[...] = packed.astype(jnp.bfloat16)
    vec[...] = jnp.concatenate(lines + [jnp.zeros((PAD - 2 * BLK_DEV, members), jnp.float32)], axis=0)
    pl.semaphore_wait(barrier, n - 1)

    def copies(k):
        peer = {"tm": (here + n - k) % n}
        return (
            pltpu.make_async_remote_copy(
                src_ref=tri, dst_ref=tri_in.at[k], send_sem=send_sem.at[0, k], recv_sem=recv_sem.at[0, k],
                device_id=peer, device_id_type=MESH,
            ),
            pltpu.make_async_remote_copy(
                src_ref=vec, dst_ref=vec_in.at[k], send_sem=send_sem.at[1, k], recv_sem=recv_sem.at[1, k],
                device_id=peer, device_id_type=MESH,
            ),
        )

    def push(k):
        @pl.when(here >= k)
        def _():
            for copy in copies(k):
                copy.start()

    steps(1, n, lambda turn: push(n - turn))

    def take(k):
        @pl.when(here + k < n)
        def _():
            for copy in copies(k):
                copy.wait_recv()
            got = tri_in[k].astype(jnp.float32)
            for h in range(BLK_DEV):
                before = acc[h]
                diag = vec_in[k, 2 * h:2 * h + 1, :]
                shift = vec_in[k, 2 * h + 1:2 * h + 2, :]
                off[h] = off[h] + jnp.sum(before * shift, axis=1, keepdims=True)
                high = before.astype(jnp.bfloat16)
                low = (before - high.astype(jnp.float32)).astype(jnp.bfloat16)
                pair = jnp.concatenate([high, low], axis=0)
                if h == 0:
                    side = jnp.where(col < row, got, 0.0).astype(jnp.bfloat16)
                    both = lax.dot_general(pair, side, NT_DIMS, preferred_element_type=jnp.float32)
                else:
                    side = jnp.where(col > row, got, 0.0).astype(jnp.bfloat16)
                    both = jnp.dot(pair, side, preferred_element_type=jnp.float32)
                acc[h] = scale * (before * diag + both[0:members, :] + both[members:, :])

    steps(1, n, take)

    def settle(k):
        @pl.when(here >= k)
        def _():
            for copy in copies(k):
                copy.wait_send()

    steps(1, n, settle)
    for h in range(BLK_DEV):
        total_ref[h] = acc[h].astype(jnp.bfloat16)
        spread = jnp.where(row == col, jnp.broadcast_to(off[h], (members, members)), 0.0)
        line = jnp.sum(spread, axis=0, keepdims=True)
        offset_ref[h] = jnp.broadcast_to(line, (16, members)).astype(jnp.bfloat16)


def apply_kernel(anom_ref, total_ref, offset_ref, smooth_ref, inc_ref, smooth, inc, sems):
    rows_dev = anom_ref.shape[1]
    tiles = 8
    tile = rows_dev // tiles
    out = []
    for i in range(tiles):
        h = i * BLK_DEV // tiles
        cut = slice(i * tile, (i + 1) * tile)
        anom = anom_ref[0, cut, :]
        smooth[0, cut, :] = jnp.dot(anom, total_ref[h], preferred_element_type=jnp.float32).astype(jnp.bfloat16)
        copy = pltpu.make_async_copy(smooth.at[:, cut, :], smooth_ref.at[:, cut, :], sems.at[i])
        copy.start()
        out.append(copy)
        part = lax.dot_general(offset_ref[h], anom, NT_DIMS, preferred_element_type=jnp.float32)
        inc[:, cut] = part[0:1, :]
    copy = pltpu.make_async_copy(inc, inc_ref, sems.at[tiles])
    copy.start()
    for copy in out + [copy]:
        copy.wait()


def body(state_anom, obs_rows, obs_weight, innovation, obs_block):
    count, members = obs_rows.shape[1:]
    n_space = lax.axis_size("space")
    n_time = lax.axis_size("tm")
    wide = members + PAD
    vmem = pl.BlockSpec(memory_space=pltpu.VMEM)
    sums, anom = pl.pallas_call(
        functools.partial(gram_kernel, n_space),
        out_shape=(
            pltpu.VMEM((wide, members), jnp.float32),
            pltpu.VMEM(state_anom.shape, state_anom.dtype),
        ),
        in_specs=[pl.BlockSpec(memory_space=pltpu.MemorySpace.HBM)] * 5,
        out_specs=(vmem, vmem),
        scratch_shapes=[
            pltpu.SemaphoreType.DMA(()),
            pltpu.VMEM((count, members), obs_rows.dtype),
            pltpu.VMEM((1, count), obs_weight.dtype),
            pltpu.VMEM((1, count), innovation.dtype),
            pltpu.VMEM((1, count), obs_block.dtype),
            pltpu.SemaphoreType.DMA((4,)),
            pltpu.VMEM((members, count), jnp.bfloat16),
            pltpu.VMEM((2 * PAD, count), jnp.bfloat16),
            pltpu.VMEM((BLK_DEV * members, count), jnp.bfloat16),
            *[pltpu.VMEM((n_space // 2, wide, members), jnp.float32)] * 4,
            pltpu.SemaphoreType.DMA((2, n_space // 2)),
            pltpu.SemaphoreType.DMA((2, n_space // 2)),
        ],
        compiler_params=pltpu.CompilerParams(collective_id=0, has_side_effects=True, vmem_limit_bytes=GRAM_GRANT),
        name="gram",
    )(obs_rows[0], obs_weight, innovation, obs_block.reshape(1, count), state_anom)
    total, offset = pl.pallas_call(
        functools.partial(factor_kernel, n_time),
        out_shape=(
            pltpu.VMEM((BLK_DEV, members, members), jnp.bfloat16),
            pltpu.VMEM((BLK_DEV, 16, members), jnp.bfloat16),
        ),
        in_specs=[vmem],
        out_specs=(vmem, vmem),
        scratch_shapes=[
            pltpu.VMEM((BLK_DEV, members, members), jnp.float32),
            pltpu.VMEM((BLK_DEV, members, 1), jnp.float32),
            pltpu.VMEM((members, members), jnp.bfloat16),
            pltpu.VMEM((PAD, members), jnp.float32),
            pltpu.VMEM((n_time, members, members), jnp.bfloat16),
            pltpu.VMEM((n_time, PAD, members), jnp.float32),
            pltpu.SemaphoreType.DMA((2, n_time)),
            pltpu.SemaphoreType.DMA((2, n_time)),
        ],
        compiler_params=pltpu.CompilerParams(collective_id=1, has_side_effects=True, vmem_limit_bytes=GRANT),
        name="factor",
    )(pltpu.with_memory_space_constraint(sums, pltpu.MemorySpace.VMEM))
    rows_dev = state_anom.shape[1]
    any_spec = pl.BlockSpec(memory_space=pl.ANY)
    return pl.pallas_call(
        apply_kernel,
        out_shape=(
            jax.ShapeDtypeStruct((1, rows_dev, members), jnp.bfloat16),
            jax.ShapeDtypeStruct((1, rows_dev), jnp.float32),
        ),
        in_specs=[vmem] * 3,
        out_specs=(any_spec, any_spec),
        scratch_shapes=[
            pltpu.VMEM((1, rows_dev, members), jnp.bfloat16),
            pltpu.VMEM((1, rows_dev), jnp.float32),
            pltpu.SemaphoreType.DMA((9,)),
        ],
        compiler_params=pltpu.CompilerParams(vmem_limit_bytes=GRANT),
        name="apply",
    )(*[pltpu.with_memory_space_constraint(x, pltpu.MemorySpace.VMEM) for x in (anom, total, offset)])


def solution(mesh):
    placed = (
        P("tm", "space", None),
        P("tm", "space", None),
        P("tm", "space"),
        P("tm", "space"),
        P("tm", "space", None),
    )
    return jax.shard_map(
        body,
        mesh=mesh,
        in_specs=placed,
        out_specs=(P("tm", "space", None), P("tm", "space")),
        check_vma=False,
    )
```
